32 devices in a mesh: row: 4 (over y, x), col: 8 (over z, core).
Axes of the slice: x: 2, y: 2, z: 4, core: 2. Of those that a mesh axis runs over, the one named last changes fastest.
Arguments:
- gradient: float32 [6144, 12288], P(('row', 'col')), may hold values from -200 to 200
Outputs:
- preconditioned: float32 [6144, 12288], P(('row', 'col'))
The draws below stay inside these ranges and needn't reach their ends.
All inputs are finite; a program needn't handle non-finite values.
Results may differ from the reference program's by a relative error of at most 0.00023.
Values sent between devices are 32-bit elements; how exact they have to be, the bound alone decides.
A program may use at most 128 MiB of HBM per device.

```python
import math
import jax
import jax.numpy as jnp
from jax import lax

D = 12288
R = 6144
BLOCK = 768
ITERS = 2


def draw_gradient(key, part):
    keys = jax.random.split(jax.random.fold_in(key, 17), 3)
    row_scale = jnp.exp(jax.random.uniform(keys[0], (R, 1), jnp.float32, 0.0, math.log(10.0)))
    col_scale = jnp.exp(jax.random.uniform(keys[1], (1, D), jnp.float32, 0.0, math.log(3.0)))
    values = jax.random.normal(keys[2], (R, D), jnp.float32) * row_scale * col_scale
    return jnp.clip(values, -200.0, 200.0).astype(jnp.float32)


def setup_inputs(seed: int = 0) -> dict:
    arg_keys = jax.random.split(jax.random.key(seed), 2)
    gradient = draw_gradient(jax.random.fold_in(arg_keys[1], 71), 0)
    return dict(gradient=gradient)


def product(first, second):
    return jnp.matmul(first, second, precision=lax.Precision.HIGHEST)

def inverse_root(gram_matrix):
    matrix_order = gram_matrix.shape[-1]
    identity = jnp.eye(matrix_order, dtype=gram_matrix.dtype)
    norm_scale = jnp.sqrt(lax.optimization_barrier(jnp.sum(gram_matrix * gram_matrix, axis=(-2, -1), keepdims=True))) + 1e-06
    iterate = gram_matrix / norm_scale
    root_now = identity
    for iteration in range(ITERS):
        factor = (5.0 * identity - iterate) * 0.25
        root_now = factor if iteration == 0 else product(root_now, factor)
        if iteration + 1 < ITERS:
            square = product(factor, factor)
            iterate = product(product(square, square), iterate)
    return root_now * norm_scale ** (-0.25)

def reference(gradient):
    block_count = D // BLOCK
    row_count = R // BLOCK
    blocks = gradient.reshape(row_count, BLOCK, block_count, BLOCK)
    left_gram = jnp.einsum('aibj,akbj->aik', blocks, blocks, precision=lax.Precision.HIGHEST) / D
    right_gram = jnp.einsum('aibj,aibk->bjk', blocks, blocks, precision=lax.Precision.HIGHEST) / D
    left_roots = inverse_root(left_gram)
    right_roots = inverse_root(right_gram)
    mixed_rows = jnp.einsum('aik,akbj->aibj', left_roots, blocks, precision=lax.Precision.HIGHEST)
    result = jnp.einsum('aibj,bjl->aibl', mixed_rows, right_roots, precision=lax.Precision.HIGHEST)
    return result.reshape(R, D)
```

```python
import jax
import jax.numpy as jnp
from jax import lax
from jax.sharding import PartitionSpec as P

D = 12288
BLOCK = 768
ITERS = 2
PART = 256


def product(first, second, precision=lax.Precision.HIGH):
    return jnp.matmul(first, second, precision=precision)


def inverse_root(gram_matrix, precision=lax.Precision.HIGH):
    matrix_order = gram_matrix.shape[-1]
    identity = jnp.eye(matrix_order, dtype=gram_matrix.dtype)
    norm_scale = jnp.sqrt(jnp.sum(gram_matrix * gram_matrix, axis=(-2, -1), keepdims=True)) + 1e-06
    iterate = gram_matrix / norm_scale
    root_now = identity
    for iteration in range(ITERS):
        factor = (5.0 * identity - iterate) * 0.25
        root_now = factor if iteration == 0 else product(root_now, factor, precision)
        if iteration + 1 < ITERS:
            square = product(factor, factor, precision)
            iterate = product(product(square, square, precision), iterate, precision)
    return root_now * norm_scale ** (-0.25)


def local_general(gradient):
    high = lax.Precision.HIGHEST
    tile_grad = lax.all_to_all(gradient, "col", split_axis=1, concat_axis=0, tiled=True)
    row_blocks = tile_grad.shape[0] // BLOCK
    col_blocks = tile_grad.shape[1] // BLOCK
    blocks = tile_grad.reshape(row_blocks, BLOCK, col_blocks, BLOCK)
    left_gram = lax.psum(jnp.einsum("aibj,akbj->aik", blocks, blocks, precision=high) / D, "col")
    right_gram = lax.psum(jnp.einsum("aibj,aibk->bjk", blocks, blocks, precision=high) / D, "row")
    left_roots = inverse_root(left_gram, high)
    right_roots = inverse_root(right_gram, high)
    mixed_rows = jnp.einsum("aik,akbj->aibj", left_roots, blocks, precision=high)
    result = jnp.einsum("aibj,bjl->aibl", mixed_rows, right_roots, precision=high)
    tile_out = result.reshape(tile_grad.shape)
    return lax.all_to_all(tile_out, "col", split_axis=0, concat_axis=1, tiled=True)


def pack(symmetric):
    def part(i, j):
        return symmetric[i * PART:(i + 1) * PART, j * PART:(j + 1) * PART]
    first = jnp.concatenate([part(0, 0), part(1, 1), part(2, 2)], axis=0)
    second = jnp.concatenate([part(0, 1), part(0, 2), part(1, 2)], axis=0)
    return first, second


def unpack(first, second):
    d0, d1, d2 = (first[i * PART:(i + 1) * PART] for i in range(3))
    o01, o02, o12 = (second[i * PART:(i + 1) * PART] for i in range(3))
    return jnp.concatenate([
        jnp.concatenate([d0, o01, o02], axis=1),
        jnp.concatenate([o01.T, d1, o12], axis=1),
        jnp.concatenate([o02.T, o12.T, d2], axis=1),
    ], axis=0)


def swap(value, axis, bits):
    size = lax.axis_size(axis)
    return lax.ppermute(value, axis, [(i, i ^ bits) for i in range(size)])


def local_grouped(gradient):
    rows = gradient.shape[0]
    group = BLOCK // rows
    width = gradient.shape[1] // group
    row_here = lax.axis_index("row")
    col_here = lax.axis_index("col")
    member = lax.rem(col_here, group)
    halves = lax.axis_size("col") // group
    order = (3, 1, 2, 0)

    blocks = {}
    grams = {}
    left_sum = None
    for k in order:
        start = (row_here ^ k) * BLOCK
        block = jnp.zeros((BLOCK, BLOCK), gradient.dtype)
        for p in range(group):
            other = member ^ p
            piece = lax.dynamic_slice(gradient, (0, other * width + start), (rows, BLOCK))
            if p:
                piece = swap(piece, "col", p)
            block = lax.dynamic_update_slice(block, piece, (other * rows, 0))
        blocks[k] = block
        right = lax.dot_general(block, block, (((0,), (0,)), ((), ())), precision=lax.Precision.HIGH)
        grams[k] = pack(right)
        left = lax.dot_general(block, block, (((1,), (1,)), ((), ())), precision=lax.Precision.HIGH)
        left_sum = left if left_sum is None else left_sum + left

    from_x = swap(grams[3][0], "row", 1)
    from_y = swap(grams[3][1], "row", 2)
    own_first = grams[0][0] + swap(grams[1][0], "row", 1) + swap(grams[2][0] + from_x, "row", 2)
    own_second = grams[0][1] + swap(grams[2][1], "row", 2) + swap(grams[1][1] + from_y, "row", 1)

    left_first, left_second = pack(left_sum)
    bits = 1
    while bits < group:
        left_first = left_first + swap(left_first, "col", bits)
        left_second = left_second + swap(left_second, "col", bits)
        bits *= 2
    left_root = inverse_root(unpack(left_first, left_second) / D)

    bits = 1
    while bits < halves:
        own_first = own_first + swap(own_first, "col", bits * group)
        own_second = own_second + swap(own_second, "col", bits * group)
        bits *= 2
    own_root = inverse_root(unpack(own_first, own_second) / D)

    root_first, root_second = pack(own_root)
    x_first, x_second = swap(root_first, "row", 1), swap(root_second, "row", 1)
    y_first, y_second = swap(root_first, "row", 2), swap(root_second, "row", 2)
    roots = {
        0: own_root,
        1: unpack(x_first, x_second),
        2: unpack(y_first, y_second),
        3: unpack(swap(x_first, "row", 2), swap(y_second, "row", 1)),
    }
    out = jnp.zeros_like(gradient)
    for k in (0, 1, 2, 3):
        mixed = product(left_root, blocks[k])
        result = product(mixed, roots[k])
        start = (row_here ^ k) * BLOCK
        for p in range(group):
            other = member ^ p
            piece = lax.dynamic_slice(result, (other * rows, 0), (rows, BLOCK))
            if p:
                piece = swap(piece, "col", p)
            out = lax.dynamic_update_slice(out, piece, (0, other * width + start))
    return out


def power_of_two(number):
    return number > 0 and number & (number - 1) == 0


def solution(mesh):
    row_total, col_total = mesh.shape["row"], mesh.shape["col"]

    def local(gradient):
        rows, columns = gradient.shape
        group = BLOCK // rows
        fits = (
            rows * group == BLOCK
            and group <= col_total
            and power_of_two(group)
            and power_of_two(col_total)
            and row_total == 4
            and columns == group * row_total * BLOCK
        )
        return local_grouped(gradient) if fits else local_general(gradient)

    in_specs = (P(("row", "col"), None),)
    out_specs = P(("row", "col"), None)
    return jax.shard_map(local, mesh=mesh, in_specs=in_specs, out_specs=out_specs, check_vma=False)
```

```python
import jax
import jax.numpy as jnp
from jax import lax
from jax.sharding import PartitionSpec as P

D = 12288
BLOCK = 768
ITERS = 2
PART = 256


def product(first, second, precision=lax.Precision.HIGH):
    return jnp.matmul(first, second, precision=precision)


def inverse_root(gram_matrix, precision=lax.Precision.HIGH):
    matrix_order = gram_matrix.shape[-1]
    identity = jnp.eye(matrix_order, dtype=gram_matrix.dtype)
    norm_scale = jnp.sqrt(jnp.sum(gram_matrix * gram_matrix, axis=(-2, -1), keepdims=True)) + 1e-06
    iterate = gram_matrix / norm_scale
    root_now = identity
    for iteration in range(ITERS):
        factor = (5.0 * identity - iterate) * 0.25
        root_now = factor if iteration == 0 else product(root_now, factor, precision)
        if iteration + 1 < ITERS:
            square = product(factor, factor, precision)
            iterate = product(product(square, square, precision), iterate, precision)
    return root_now * norm_scale ** (-0.25)


def local_general(gradient):
    high = lax.Precision.HIGHEST
    tile_grad = lax.all_to_all(gradient, "col", split_axis=1, concat_axis=0, tiled=True)
    row_blocks = tile_grad.shape[0] // BLOCK
    col_blocks = tile_grad.shape[1] // BLOCK
    blocks = tile_grad.reshape(row_blocks, BLOCK, col_blocks, BLOCK)
    left_gram = lax.psum(jnp.einsum("aibj,akbj->aik", blocks, blocks, precision=high) / D, "col")
    right_gram = lax.psum(jnp.einsum("aibj,aibk->bjk", blocks, blocks, precision=high) / D, "row")
    left_roots = inverse_root(left_gram, high)
    right_roots = inverse_root(right_gram, high)
    mixed_rows = jnp.einsum("aik,akbj->aibj", left_roots, blocks, precision=high)
    result = jnp.einsum("aibj,bjl->aibl", mixed_rows, right_roots, precision=high)
    tile_out = result.reshape(tile_grad.shape)
    return lax.all_to_all(tile_out, "col", split_axis=0, concat_axis=1, tiled=True)


def pack(symmetric):
    def part(i, j):
        return symmetric[i * PART:(i + 1) * PART, j * PART:(j + 1) * PART]
    first = jnp.concatenate([part(0, 0), part(1, 1), part(2, 2)], axis=0)
    second = jnp.concatenate([part(0, 1), part(0, 2), part(1, 2)], axis=0)
    return first, second


def unpack(first, second):
    d0, d1, d2 = (first[i * PART:(i + 1) * PART] for i in range(3))
    o01, o02, o12 = (second[i * PART:(i + 1) * PART] for i in range(3))
    return jnp.concatenate([
        jnp.concatenate([d0, o01, o02], axis=1),
        jnp.concatenate([o01.T, d1, o12], axis=1),
        jnp.concatenate([o02.T, o12.T, d2], axis=1),
    ], axis=0)


def swap(value, axis, bits):
    size = lax.axis_size(axis)
    return lax.ppermute(value, axis, [(i, i ^ bits) for i in range(size)])


def local_grouped(gradient):
    rows = gradient.shape[0]
    group = BLOCK // rows
    width = gradient.shape[1] // group
    row_here = lax.axis_index("row")
    col_here = lax.axis_index("col")
    member = lax.rem(col_here, group)
    halves = lax.axis_size("col") // group
    order = (3, 1, 2, 0)

    def reorder(symmetric):
        for turn in range(2):
            bits = 1
            while bits < group:
                parts = [symmetric[(p ^ bits) * rows:((p ^ bits) + 1) * rows] for p in range(group)]
                symmetric = jnp.where((member & bits) != 0, jnp.concatenate(parts, axis=0), symmetric)
                bits *= 2
            symmetric = symmetric.T
        return symmetric

    starts = {k: (row_here ^ k) * BLOCK for k in order}

    def fetch(k):
        pieces = []
        for p in range(group):
            piece = lax.dynamic_slice(gradient, (0, (member ^ p) * width + starts[k]), (rows, BLOCK))
            pieces.append(swap(piece, "col", p) if p else piece)
        return pieces

    barrier = lax.optimization_barrier
    blocks = {}
    arrived = {k: fetch(k) for k in order[:2]}
    left_sum = None
    moved = ()
    for step, k in enumerate(order):
        pieces = arrived[k]
        if step + 2 < len(order):
            later = order[step + 2]
            pieces, starts[later] = barrier((pieces, starts[later]))
            arrived[later] = fetch(later)
        if k == 2:
            pieces, (from_x, from_y) = barrier((pieces, (from_x, from_y)))
        if k == 0:
            pieces, moved = barrier((pieces, moved))
        block = jnp.concatenate(pieces, axis=0)
        right = lax.dot_general(block, block, (((0,), (0,)), ((), ())), precision=lax.Precision.HIGH)
        (first, second), block = barrier((pack(right), block))
        left = lax.dot_general(block, block, (((1,), (1,)), ((), ())), precision=lax.Precision.HIGH)
        left_sum = left if left_sum is None else left_sum + left
        blocks[k] = block
        if k == 3:
            from_x, from_y = swap(first, "row", 1), swap(second, "row", 2)
        elif k == 1:
            moved = (swap(first, "row", 1), swap(second + from_y, "row", 1))
        elif k == 2:
            last = (swap(first + from_x, "row", 2), swap(second, "row", 2))
        else:
            left_sum, last = barrier((left_sum, last))
            own_first = first + moved[0] + last[0]
            own_second = second + moved[1] + last[1]

    left_first, left_second = pack(reorder(left_sum))
    bits = 1
    while bits < group:
        left_first = left_first + swap(left_first, "col", bits)
        left_second = left_second + swap(left_second, "col", bits)
        bits *= 2
    left_root = reorder(inverse_root(unpack(left_first, left_second) / D))

    bits = 1
    while bits < halves:
        own_first = own_first + swap(own_first, "col", bits * group)
        own_second = own_second + swap(own_second, "col", bits * group)
        bits *= 2
    own_root = inverse_root(unpack(own_first, own_second) / D)

    root_first, root_second = pack(own_root)
    x_first, x_second = swap(root_first, "row", 1), swap(root_second, "row", 1)
    y_first, y_second = swap(root_first, "row", 2), swap(root_second, "row", 2)
    roots = {
        0: own_root,
        1: unpack(x_first, x_second),
        2: unpack(y_first, y_second),
        3: unpack(swap(x_first, "row", 2), swap(y_second, "row", 1)),
    }
    out = jnp.zeros_like(gradient)
    for k in (0, 1, 2, 3):
        mixed = product(left_root, blocks[k])
        result = product(mixed, roots[k])
        start = (row_here ^ k) * BLOCK
        for p in range(group):
            other = member ^ p
            piece = result[p * rows:(p + 1) * rows]
            if p:
                piece = swap(piece, "col", p)
            out = lax.dynamic_update_slice(out, piece, (0, other * width + start))
    return out


def power_of_two(number):
    return number > 0 and number & (number - 1) == 0


def solution(mesh):
    row_total, col_total = mesh.shape["row"], mesh.shape["col"]

    def local(gradient):
        rows, columns = gradient.shape
        group = BLOCK // rows
        fits = (
            rows * group == BLOCK
            and group <= col_total
            and power_of_two(group)
            and power_of_two(col_total)
            and row_total == 4
            and columns == group * row_total * BLOCK
        )
        return local_grouped(gradient) if fits else local_general(gradient)

    in_specs = (P(("row", "col"), None),)
    out_specs = P(("row", "col"), None)
    return jax.shard_map(local, mesh=mesh, in_specs=in_specs, out_specs=out_specs, check_vma=False)
```

```python
import jax
import jax.numpy as jnp
from jax import lax
from jax.sharding import PartitionSpec as P

D = 12288
BLOCK = 768
ITERS = 2
PART = 256


def product(first, second, precision=lax.Precision.HIGH):
    return jnp.matmul(first, second, precision=precision)


def inverse_root(gram_matrix, precision=lax.Precision.HIGH):
    matrix_order = gram_matrix.shape[-1]
    identity = jnp.eye(matrix_order, dtype=gram_matrix.dtype)
    norm_scale = jnp.sqrt(jnp.sum(gram_matrix * gram_matrix, axis=(-2, -1), keepdims=True)) + 1e-06
    iterate = gram_matrix / norm_scale
    root_now = identity
    for iteration in range(ITERS):
        factor = (5.0 * identity - iterate) * 0.25
        root_now = factor if iteration == 0 else product(root_now, factor, precision)
        if iteration + 1 < ITERS:
            square = product(factor, factor, precision)
            iterate = product(product(square, square, precision), iterate, precision)
    return root_now * norm_scale ** (-0.25)


def local_general(gradient):
    high = lax.Precision.HIGHEST
    tile_grad = lax.all_to_all(gradient, "col", split_axis=1, concat_axis=0, tiled=True)
    row_blocks = tile_grad.shape[0] // BLOCK
    col_blocks = tile_grad.shape[1] // BLOCK
    blocks = tile_grad.reshape(row_blocks, BLOCK, col_blocks, BLOCK)
    left_gram = lax.psum(jnp.einsum("aibj,akbj->aik", blocks, blocks, precision=high) / D, "col")
    right_gram = lax.psum(jnp.einsum("aibj,aibk->bjk", blocks, blocks, precision=high) / D, "row")
    left_roots = inverse_root(left_gram, high)
    right_roots = inverse_root(right_gram, high)
    mixed_rows = jnp.einsum("aik,akbj->aibj", left_roots, blocks, precision=high)
    result = jnp.einsum("aibj,bjl->aibl", mixed_rows, right_roots, precision=high)
    tile_out = result.reshape(tile_grad.shape)
    return lax.all_to_all(tile_out, "col", split_axis=0, concat_axis=1, tiled=True)


def pack(symmetric):
    def part(i, j):
        return symmetric[i * PART:(i + 1) * PART, j * PART:(j + 1) * PART]
    first = jnp.concatenate([part(0, 0), part(1, 1), part(2, 2)], axis=0)
    second = jnp.concatenate([part(0, 1), part(0, 2), part(1, 2)], axis=0)
    return first, second


def unpack(first, second):
    d0, d1, d2 = (first[i * PART:(i + 1) * PART] for i in range(3))
    o01, o02, o12 = (second[i * PART:(i + 1) * PART] for i in range(3))
    return jnp.concatenate([
        jnp.concatenate([d0, o01, o02], axis=1),
        jnp.concatenate([o01.T, d1, o12], axis=1),
        jnp.concatenate([o02.T, o12.T, d2], axis=1),
    ], axis=0)


def swap(value, axis, bits):
    size = lax.axis_size(axis)
    return lax.ppermute(value, axis, [(i, i ^ bits) for i in range(size)])


def local_grouped(gradient):
    rows = gradient.shape[0]
    group = BLOCK // rows
    width = gradient.shape[1] // group
    row_here = lax.axis_index("row")
    col_here = lax.axis_index("col")
    member = lax.rem(col_here, group)
    halves = lax.axis_size("col") // group
    order = (3, 1, 2, 0)

    def reorder(symmetric):
        for turn in range(2):
            bits = 1
            while bits < group:
                parts = [symmetric[(p ^ bits) * rows:((p ^ bits) + 1) * rows] for p in range(group)]
                symmetric = jnp.where((member & bits) != 0, jnp.concatenate(parts, axis=0), symmetric)
                bits *= 2
            symmetric = symmetric.T
        return symmetric

    starts = {k: (row_here ^ k) * BLOCK for k in order}

    def fetch(k):
        pieces = []
        for p in range(group):
            piece = lax.dynamic_slice(gradient, (0, (member ^ p) * width + starts[k]), (rows, BLOCK))
            pieces.append(swap(piece, "col", p) if p else piece)
        return pieces

    barrier = lax.optimization_barrier
    blocks = {}
    arrived = {order[0]: fetch(order[0])}
    arrived[order[0]][-1 if group == 1 else 1], starts[order[1]] = barrier(
        (arrived[order[0]][-1 if group == 1 else 1], starts[order[1]]))
    arrived[order[1]] = fetch(order[1])
    left_sum = None
    moved = ()
    for step, k in enumerate(order):
        pieces = arrived[k]
        if step + 2 < len(order):
            later = order[step + 2]
            pieces, starts[later] = barrier((pieces, starts[later]))
            arrived[later] = fetch(later)
        if k == 2:
            pieces, (from_x, from_y) = barrier((pieces, (from_x, from_y)))
        if k == 0:
            pieces, moved = barrier((pieces, moved))
        block = jnp.concatenate(pieces, axis=0)
        right = lax.dot_general(block, block, (((0,), (0,)), ((), ())), precision=lax.Precision.HIGH)
        (first, second), block = barrier((pack(right), block))
        left = lax.dot_general(block, block, (((1,), (1,)), ((), ())), precision=lax.Precision.HIGH)
        left_sum = left if left_sum is None else left_sum + left
        blocks[k] = block
        if k == 3:
            from_x, from_y = swap(first, "row", 1), swap(second, "row", 2)
        elif k == 1:
            moved = (swap(first, "row", 1), swap(second + from_y, "row", 1))
        elif k == 2:
            last = (swap(first + from_x, "row", 2), swap(second, "row", 2))
        else:
            left_sum, last = barrier((left_sum, last))
            own_first = first + moved[0] + last[0]
            own_second = second + moved[1] + last[1]

    left_first, left_second = pack(reorder(left_sum))
    bits = group // 2
    while bits >= 1:
        left_first = left_first + swap(left_first, "col", bits)
        left_second = left_second + swap(left_second, "col", bits)
        bits //= 2
    left_root = reorder(inverse_root(unpack(left_first, left_second) / D))

    bits = 1
    while bits < halves:
        own_first = own_first + swap(own_first, "col", bits * group)
        own_second = own_second + swap(own_second, "col", bits * group)
        bits *= 2
    (own_first, own_second), left_root = barrier(((own_first, own_second), left_root))
    own_root = inverse_root(unpack(own_first, own_second) / D)

    root_first, root_second = pack(own_root)
    x_first, x_second = swap(root_first, "row", 1), swap(root_second, "row", 1)
    y_first, y_second = swap(root_first, "row", 2), swap(root_second, "row", 2)
    roots = {
        0: own_root,
        1: unpack(x_first, x_second),
        2: unpack(y_first, y_second),
        3: unpack(swap(x_first, "row", 2), swap(y_second, "row", 1)),
    }
    out = jnp.zeros_like(gradient)
    for k in (0, 1, 2, 3):
        mixed = product(left_root, blocks[k])
        result = product(mixed, roots[k])
        start = (row_here ^ k) * BLOCK
        for p in range(group):
            other = member ^ p
            piece = result[p * rows:(p + 1) * rows]
            if p:
                piece = swap(piece, "col", p)
            out = lax.dynamic_update_slice(out, piece, (0, other * width + start))
    return out


def power_of_two(number):
    return number > 0 and number & (number - 1) == 0


def solution(mesh):
    row_total, col_total = mesh.shape["row"], mesh.shape["col"]

    def local(gradient):
        rows, columns = gradient.shape
        group = BLOCK // rows
        fits = (
            rows * group == BLOCK
            and group <= col_total
            and power_of_two(group)
            and power_of_two(col_total)
            and row_total == 4
            and columns == group * row_total * BLOCK
        )
        return local_grouped(gradient) if fits else local_general(gradient)

    in_specs = (P(("row", "col"), None),)
    out_specs = P(("row", "col"), None)
    return jax.shard_map(local, mesh=mesh, in_specs=in_specs, out_specs=out_specs, check_vma=False)
```
